32 devices in a mesh: dp: 16 (over z, x, core), ctx: 2 (over y).
Axes of the slice: x: 2, y: 2, z: 4, core: 2. Of those that a mesh axis runs over, the one named last changes fastest.
Arguments:
- queries: bfloat16 [16, 512, 2048], P('dp', 'ctx'), may hold values from -48 to 48
- key_store: bfloat16 [16, 512, 2048], P('dp', 'ctx'), may hold values from -4 to 4
- value_store: bfloat16 [16, 512, 2048], P('dp', 'ctx'), may hold values from -5 to 5
- kv_exponents: int32 [16, 4, 16], P('dp', 'ctx'), may hold values from -1 to 1
- valid_length: int32 [16], P('dp'), may hold values from 64 to 512, as said below
- round_index: int32 [1], replicated, may hold values from 0 to 63
- out_grad: bfloat16 [16, 512, 2048], P('dp', None, 'ctx'), may hold values from -6 to 6
- params: bfloat16 [16, 2048, 2048], P('dp', None, 'ctx'), may hold values from -6 to 6
- tracker: bfloat16 [16, 2048, 2048], P('dp', None, 'ctx'), may hold values from -6 to 6
- old_grad: bfloat16 [16, 2048, 2048], P('dp', None, 'ctx'), may hold values from -6 to 6
Outputs:
- new_params: bfloat16 [16, 2048, 2048], P('dp', None, 'ctx')
- new_tracker: bfloat16 [16, 2048, 2048], P('dp', None, 'ctx')
The draws below stay inside these ranges and needn't reach their ends.
Inputs may be any that keep to these rules, and one draw needn't show every extreme that they name: `valid_length`: every draw has a replica whose clip fills all 512 positions.
All inputs are finite; a program needn't handle non-finite values.
Results may differ from the reference program's by a relative error of at most 0.0053.
Values may be sent and summed in bfloat16 or wider, within the bound.
A program may use at most 128 MiB of HBM per device.

```python
import jax
import jax.numpy as jnp
from jax import lax

D = 2048
HEADS = 16
HD = 128
KBLK = 128
REPLICAS = 16
SEQ = 512
N_DP = 16


def draw_base(key):
    base = jax.random.fold_in(key, 17)
    query_key, key_key = jax.random.split(base, 2)
    full_shape = (REPLICAS, SEQ, HEADS * HD)
    queries = jax.random.truncated_normal(query_key, -4.0, 4.0, full_shape, jnp.float32)
    key_rows = jax.random.truncated_normal(key_key, -4.0, 4.0, full_shape, jnp.float32)
    return (queries, key_rows)


def draw_queries(key, part):
    queries, key_rows = draw_base(key)
    return queries.astype(jnp.bfloat16)


def draw_key_store(key, part):
    queries, key_rows = draw_base(key)
    return key_rows.astype(jnp.bfloat16)


def draw_valid_length(key, part):
    base = jax.random.fold_in(key, 29)
    length_key, pick_key = jax.random.split(base, 2)
    lengths = jax.random.randint(length_key, (REPLICAS,), SEQ // 8, SEQ + 1)
    longest = jax.random.randint(pick_key, (), 0, REPLICAS)
    return jnp.where(jnp.arange(REPLICAS) == longest, SEQ, lengths).astype(jnp.int32)


def touch_ends(array, own_key, least, largest):
    longest = array.shape.index(max(array.shape))
    spots = []
    for shift in (0, 1):
        where = [jax.random.randint(jax.random.fold_in(own_key, axis), (), 0, length) for axis, length in enumerate(array.shape)]
        where[longest] = (where[longest] + shift) % array.shape[longest]
        spots.append(tuple(where))
    return array.at[spots[0]].set(least).at[spots[1]].set(largest)


def shard_levels(rng, shape, pieces, low, top_value):
    level = 1.0
    for position, blocks in pieces:
        steps = jax.random.uniform(jax.random.fold_in(jax.random.fold_in(rng, 6), position), (blocks,), jnp.float32, low / len(pieces), top_value / len(pieces))
        level = level * jnp.repeat(jnp.exp(steps), shape[position] // blocks).reshape((-1,) + (1,) * (len(shape) - 1 - position))
    return level


def scatter_about(stream_key, extent, width, limit, pieces=(), kind=jnp.bfloat16):
    loudness = shard_levels(stream_key, extent, pieces, -0.22, 0.18) if pieces else 1.0
    array = jax.random.normal(stream_key, extent, jnp.float32) * width * loudness
    return jnp.minimum(jnp.maximum(array, -limit), limit).astype(kind)


def setup_inputs(seed: int = 0) -> dict:
    seeds = jax.random.split(jax.random.key(seed), 11)
    return {
        "queries": draw_queries(jax.random.fold_in(seeds[10], 71), 0),
        "key_store": draw_key_store(jax.random.fold_in(seeds[10], 71), 0),
        "value_store": scatter_about(seeds[2], (REPLICAS, SEQ, HEADS * HD), 1.0, 5.0, ((0, 16), (1, 2))),
        "kv_exponents": touch_ends(jax.random.randint(seeds[3], (REPLICAS, SEQ // KBLK, HEADS), -1, 2), jax.random.fold_in(seeds[3], 1), -1, 1).astype(jnp.int32),
        "valid_length": draw_valid_length(jax.random.fold_in(seeds[10], 71), 0),
        "round_index": jax.random.randint(seeds[5], (1,), 0, 64).astype(jnp.int32),
        "out_grad": scatter_about(seeds[6], (REPLICAS, SEQ, D), 1.0, 6.0, ((0, 16), (2, 2))),
        "params": scatter_about(seeds[7], (REPLICAS, HEADS * HD, D), 1.0, 6.0, ((0, 16), (2, 2))),
        "tracker": scatter_about(seeds[8], (REPLICAS, HEADS * HD, D), 1.0, 6.0, ((0, 16), (2, 2))),
        "old_grad": scatter_about(seeds[9], (REPLICAS, HEADS * HD, D), 1.0, 6.0, ((0, 16), (2, 2))),
    }


step_size = 0.1
masked_score = -1e30


def dequantize(stored, exponents):
    factor = jnp.exp2(exponents.astype(jnp.float32))
    factor = jnp.repeat(jnp.repeat(factor, KBLK, axis=0), HD, axis=1)
    return (stored.astype(jnp.float32) * factor).astype(jnp.bfloat16)


def attend(query_rows, key_rows, value_rows, length):
    positions = jnp.arange(SEQ)
    allowed = (positions[None, :] <= positions[:, None]) & (positions[None, :] < length)
    query_heads = query_rows.astype(jnp.float32).reshape(SEQ, HEADS, HD)
    key_heads = key_rows.astype(jnp.float32).reshape(SEQ, HEADS, HD)
    value_heads = value_rows.astype(jnp.float32).reshape(SEQ, HEADS, HD)
    scores = jnp.einsum("qhd,khd->hqk", query_heads, key_heads) * (HD ** -0.5)
    scores = jnp.where(allowed[None], scores, masked_score)
    row_top = jnp.max(scores, axis=-1, keepdims=True)
    weights = jnp.where(allowed[None], jnp.exp(scores - row_top), 0.0)
    row_total = jnp.sum(weights, axis=-1)
    rounded = lax.optimization_barrier(weights.astype(jnp.bfloat16)).astype(jnp.float32)
    attended = jnp.einsum("hqk,khd->qhd", rounded, value_heads) / jnp.transpose(row_total)[:, :, None]
    return attended.reshape(SEQ, HEADS * HD).astype(jnp.bfloat16)


def reference(queries, key_store, value_store, kv_exponents, valid_length, round_index, out_grad, params, tracker, old_grad):
    levels = N_DP.bit_length() - 1
    bit_now = (round_index[0] % levels).astype(jnp.int32)

    def replica(replica_id):
        partner = jnp.bitwise_xor(replica_id, jnp.left_shift(jnp.int32(1), bit_now)).astype(jnp.int32)
        length = valid_length[replica_id]
        key_rows = dequantize(key_store[replica_id], kv_exponents[replica_id])
        value_rows = dequantize(value_store[replica_id], kv_exponents[replica_id])
        attended = attend(queries[replica_id], key_rows, value_rows, length)
        live_rows = jnp.arange(SEQ)[:, None] < length
        masked = jnp.where(live_rows, out_grad[replica_id], jnp.zeros((), jnp.bfloat16))
        grad_new = jnp.dot(attended.T, masked, preferred_element_type=jnp.float32)
        tracker_sum = 0.5 * (tracker[replica_id].astype(jnp.float32) + tracker[partner].astype(jnp.float32)) + grad_new - old_grad[replica_id].astype(jnp.float32)
        tracker_next = tracker_sum.astype(jnp.bfloat16)
        params_next = (0.5 * (params[replica_id].astype(jnp.float32) + params[partner].astype(jnp.float32)) - step_size * tracker_next.astype(jnp.float32)).astype(jnp.bfloat16)
        return params_next, tracker_next

    new_params, new_tracker = lax.map(replica, jnp.arange(REPLICAS, dtype=jnp.int32))
    return new_params, new_tracker
```

```python
import functools

import jax
import jax.numpy as jnp
from jax import lax
from jax.experimental import pallas as pl
from jax.experimental.pallas import tpu as pltpu
from jax.sharding import PartitionSpec as P


HEADS = 16
HD = 128
KBLK = 128
QROWS = 256
LAST_ROWS = 256
VMEM_LIMIT = 40 * 2**20
FLUSH_LIMIT = 16 * 2**20


step_size = 0.1
masked_score = -1e30


def from_partner(value, axis, bit):
    mask = 2**bit
    pairs = [(source, source ^ mask) for source in range(lax.axis_size(axis))]
    return lax.ppermute(value, axis, pairs)


def contract_rows(left_rows, right_rows):
    return lax.dot_general(
        left_rows, right_rows, (((0,), (0,)), ((), ())), preferred_element_type=jnp.float32
    )


def from_other(block):
    return lax.ppermute(block, "ctx", [(0, 1), (1, 0)])


def in_order(own, other, axis):
    first = lax.axis_index("ctx") == 0
    return jnp.concatenate(
        (jnp.where(first, own, other), jnp.where(first, other, own)), axis=axis
    )


def gather_ctx(block, axis):
    if lax.axis_size("ctx") != 2:
        return lax.all_gather(block, "ctx", axis=axis, tiled=True)
    return in_order(block, from_other(block), axis)


def rows_to_heads(block, group, groups):
    if lax.axis_size("ctx") != 2:
        return lax.all_to_all(block, "ctx", split_axis=1, concat_axis=0, tiled=True)
    width = block.shape[1] // (2 * groups)
    mine = lax.axis_index("ctx")
    kept = lax.dynamic_slice_in_dim(block, (mine * groups + group) * width, width, 1)
    sent = lax.dynamic_slice_in_dim(block, ((1 - mine) * groups + group) * width, width, 1)
    return in_order(kept, from_other(sent), 0)


def attend_kernel(step_heads, meta, scales, q_ref, k_ref, v_ref, out_ref):
    length = meta[0]
    seq = k_ref.shape[0]
    for local in range(step_heads):
        head = meta[1] + pl.program_id(0) * step_heads + local
        cols = pl.ds(local * HD, HD)

        def scaled(ref):
            return jnp.concatenate(
                [
                    (
                        ref[pl.ds(block * KBLK, KBLK), cols].astype(jnp.float32)
                        * scales[block, head]
                    ).astype(jnp.bfloat16)
                    for block in range(seq // KBLK)
                ],
                axis=0,
            )

        keys, values = scaled(k_ref), scaled(v_ref)
        for row0 in range(0, seq, QROWS):
            reach = row0 + QROWS
            scores = lax.dot_general(
                q_ref[pl.ds(row0, QROWS), cols],
                keys[:reach],
                (((1,), (1,)), ((), ())),
                preferred_element_type=jnp.float32,
            ) * (HD ** (-0.5))
            query_pos = row0 + lax.broadcasted_iota(jnp.int32, scores.shape, 0)
            key_pos = lax.broadcasted_iota(jnp.int32, scores.shape, 1)
            allowed = (key_pos <= query_pos) & (key_pos < length)
            scores = jnp.where(allowed, scores, masked_score)
            top = jnp.max(scores, axis=-1, keepdims=True)
            weights = jnp.exp(scores - top)
            total = jnp.sum(weights, axis=-1, keepdims=True)
            weighted = jnp.dot(
                weights.astype(jnp.bfloat16), values[:reach], preferred_element_type=jnp.float32
            )
            out_ref[pl.ds(row0, QROWS), cols] = (weighted / total).astype(jnp.bfloat16)


def attend(queries, keys, values, scales, length, first_head):
    seq, width = queries.shape
    heads = width // HD
    step_heads = 2 if heads % 2 == 0 and seq <= 512 else 1
    meta = jnp.stack((length, first_head)).astype(jnp.int32)
    spec = pl.BlockSpec((seq, step_heads * HD), lambda h: (0, h))
    smem = pl.BlockSpec(memory_space=pltpu.SMEM)
    return pl.pallas_call(
        functools.partial(attend_kernel, step_heads),
        grid=(heads // step_heads,),
        in_specs=[smem, smem, spec, spec, spec],
        out_specs=spec,
        out_shape=jax.ShapeDtypeStruct((seq, width), jnp.bfloat16),
        cost_estimate=pl.CostEstimate(
            flops=4 * seq * seq * width,
            bytes_accessed=8 * seq * width,
            transcendentals=seq * seq * heads,
        ),
    )(meta, scales, queries, keys, values)


def average_kernel(own_ref, peer_ref, tracker_ref, *rest):
    out_ref = rest[-1]
    out_ref[...] = (
        0.5 * (own_ref[...].astype(jnp.float32) + peer_ref[...].astype(jnp.float32))
        - step_size * tracker_ref[...].astype(jnp.float32)
    ).astype(jnp.bfloat16)


def average_rows(own, peer_rows, new_tracker, start, filled=None):
    rows, cols = peer_rows.shape
    tile = LAST_ROWS
    here = pl.BlockSpec((tile, cols), lambda i: (i + start // tile, 0))
    operands = [own, peer_rows, new_tracker]
    peer_spec = pl.BlockSpec((tile, cols), lambda i: (i, 0))
    if rows == tile:
        peer_spec = pl.BlockSpec(memory_space=pltpu.VMEM)
    specs = [here, peer_spec, here]
    aliases = {}
    if filled is not None:
        operands.append(filled)
        specs.append(pl.BlockSpec(memory_space=pl.ANY))
        aliases = {3: 0}
    return pl.pallas_call(
        average_kernel,
        grid=(rows // tile,),
        in_specs=specs,
        out_specs=here,
        out_shape=jax.ShapeDtypeStruct(own.shape, jnp.bfloat16),
        input_output_aliases=aliases,
        cost_estimate=pl.CostEstimate(
            flops=4 * rows * cols, bytes_accessed=8 * rows * cols, transcendentals=0
        ),
    )(*operands)


PAIR = 2
GROUP = PAIR * HD
MESH = pl.DeviceIdType.MESH


def scaled_rows(ref, scales, head, cols):
    return jnp.concatenate(
        [
            (
                ref[pl.ds(block * KBLK, KBLK), cols].astype(jnp.float32) * scales[block, head]
            ).astype(jnp.bfloat16)
            for block in range(ref.shape[0] // KBLK)
        ],
        axis=0,
    )


def attend_columns(queries, keys, values, allowed):
    scores = lax.dot_general(
        keys, queries, (((1,), (1,)), ((), ())), preferred_element_type=jnp.float32
    ) * (HD ** (-0.5))
    scores = jnp.where(allowed, scores, masked_score)
    top = jnp.max(scores, axis=0, keepdims=True)
    weights = jnp.exp(scores - top)
    total = jnp.sum(weights, axis=0, keepdims=True)
    return contract_rows(values, weights.astype(jnp.bfloat16)), top, total


def core_pair_kernel(
    length_ref, scales, query_hbm, key_hbm, value_hbm, grad_hbm, tracker_hbm, params_hbm, old_hbm,
    new_tracker_ref, new_params_ref,
    queries, keys, values, masked, tracker, params, old, peer_tracker, peer_params,
    peer_queries, low, high, part, stats, own, own_stats,
    load_sem, trade_send, trade_recv, query_send, query_recv, low_send, low_recv,
    high_send, high_recv, part_send, part_recv, stats_send, stats_recv,
):
    rows = queries.shape[0]
    groups = queries.shape[1] // GROUP
    side = lax.axis_index("ctx")
    place = lax.axis_index("dp")
    across = {"ctx": 1 - side}
    partner = {"dp": place + 1 - 2 * (place % 2)}
    length = length_ref[0]

    def span(group):
        return pl.ds(pl.multiple_of(group * GROUP, GROUP), GROUP)

    def remote(source, target, send, recv, device):
        return pltpu.make_async_remote_copy(
            src_ref=source, dst_ref=target, send_sem=send, recv_sem=recv,
            device_id=device, device_id_type=MESH,
        )

    def trade_tracker(group):
        here = span(group)
        return remote(tracker_hbm.at[here], peer_tracker.at[here],
                      trade_send.at[0, group], trade_recv.at[0, group], partner)

    def trade_params(group):
        here = span(group)
        return remote(params_hbm.at[here], peer_params.at[here],
                      trade_send.at[1, group], trade_recv.at[1, group], partner)

    def move_queries(group):
        here = span(group)
        return remote(query_hbm.at[:, here], peer_queries.at[:, here],
                      query_send.at[group], query_recv.at[group], across)

    def move_low(group):
        here = span(group)
        return remote(low.at[here], low.at[here], low_send.at[group], low_recv.at[group], across)

    def move_high(group):
        here = span(group)
        return remote(high.at[here], high.at[here], high_send.at[group], high_recv.at[group],
                      across)

    def move_part(group):
        here = span(group)
        return remote(part.at[here], part.at[here], part_send.at[group], part_recv.at[group],
                      across)

    def move_stats(group):
        return remote(stats.at[group], stats.at[group], stats_send.at[group],
                      stats_recv.at[group], across)

    loads = [
        pltpu.make_async_copy(source, target, load_sem.at[index])
        for index, (source, target) in enumerate((
            (query_hbm, queries), (key_hbm, keys), (value_hbm, values), (grad_hbm, masked),
            (tracker_hbm, tracker), (params_hbm, params), (old_hbm, old),
        ))
    ]
    for load in loads[:3]:
        load.start()
    barrier = pltpu.get_barrier_semaphore()
    for device in (across, partner):
        pl.semaphore_signal(barrier, inc=1, device_id=device, device_id_type=MESH)
    pl.semaphore_wait(barrier, 2)

    def each(first, last, body):
        def step(group, carry):
            body(group)
            return carry

        lax.fori_loop(first, last, step, 0)

    @pl.when(side == 1)
    def _():
        each(0, groups, lambda group: move_queries(group).start())

    def start_trades(group):
        trade_tracker(group).start()
        trade_params(group).start()

    each(0, groups, start_trades)
    for load in loads[3:]:
        load.start()
    for load in loads[:3]:
        load.wait()

    key_pos = lax.broadcasted_iota(jnp.int32, (rows, rows), 0)
    query_pos = lax.broadcasted_iota(jnp.int32, (rows, rows), 1)

    def heads_of(group):
        for local in range(PAIR):
            head = group * PAIR + local
            yield local, head, pl.ds(pl.multiple_of(head * HD, HD), HD)

    def own_keys(head, cols):
        return scaled_rows(keys, scales, head, cols), scaled_rows(values, scales, head, cols)

    def mask_grad():
        loads[3].wait()
        for block in range(masked.shape[0] // KBLK):
            here = pl.ds(block * KBLK, KBLK)
            position = block * KBLK + lax.broadcasted_iota(jnp.int32, (KBLK, masked.shape[1]), 0)
            masked[here] = jnp.where(
                position < length, masked[here].astype(jnp.float32), 0.0
            ).astype(jnp.bfloat16)

    def update(group):
        here = span(group)
        trade_tracker(group).wait_recv()
        trade_params(group).wait_recv()
        grad = jnp.dot(low[here], masked[pl.ds(0, rows)], preferred_element_type=jnp.float32)
        grad += jnp.dot(high[here], masked[pl.ds(rows, rows)], preferred_element_type=jnp.float32)
        new_tracker = (
            0.5 * (tracker[here].astype(jnp.float32) + peer_tracker[here].astype(jnp.float32))
            + grad
            - old[here].astype(jnp.float32)
        ).astype(jnp.bfloat16)
        new_tracker_ref[here] = new_tracker
        new_params_ref[here] = (
            0.5 * (params[here].astype(jnp.float32) + peer_params[here].astype(jnp.float32))
            - step_size * new_tracker.astype(jnp.float32)
        ).astype(jnp.bfloat16)

    def wait_rest():
        for load in loads[4:]:
            load.wait()

    @pl.when(side == 0)
    def _():
        causal = (key_pos <= query_pos) & (key_pos < length)
        live = key_pos < length

        def make_low(group):
            for _, head, cols in heads_of(group):
                head_keys, head_values = own_keys(head, cols)
                weighted, _, total = attend_columns(
                    queries[:, cols], head_keys, head_values, causal
                )
                low[cols] = (weighted / total).astype(jnp.bfloat16)

        def make_part(group):
            move_queries(group).wait_recv()
            for local, head, cols in heads_of(group):
                head_keys, head_values = own_keys(head, cols)
                weighted, top, total = attend_columns(
                    peer_queries[:, cols], head_keys, head_values, live
                )
                part[cols] = (weighted / total).astype(jnp.bfloat16)
                stats[group, pl.ds(local, 1)] = top
                stats[group, pl.ds(PAIR + local, 1)] = total

        def send_part(group):
            move_part(group).start()
            move_stats(group).start()

        def step(group):
            make_part(group)
            make_low(group + 1)
            send_part(group)

        make_low(0)
        move_low(0).start()
        each(0, groups - 1, step)
        make_part(groups - 1)
        mask_grad()
        send_part(groups - 1)
        each(1, groups, lambda group: move_low(group).start())
        wait_rest()

        def finish(group):
            move_high(group).wait_recv()
            update(group)

        each(0, groups, finish)

        def drain(group):
            move_low(group).wait_send()
            move_part(group).wait_send()
            move_stats(group).wait_send()

        each(0, groups, drain)

    @pl.when(side == 1)
    def _():
        causal = (key_pos <= query_pos) & (key_pos + rows < length)

        def make_own(group):
            for local, head, cols in heads_of(group):
                head_keys, head_values = own_keys(head, cols)
                weighted, top, total = attend_columns(
                    queries[:, cols], head_keys, head_values, causal
                )
                own[cols] = weighted
                own_stats[group, pl.ds(local, 1)] = top
                own_stats[group, pl.ds(PAIR + local, 1)] = total

        def make_high(group):
            move_part(group).wait_recv()
            move_stats(group).wait_recv()
            for local, _, cols in heads_of(group):
                part_top = stats[group, pl.ds(local, 1)]
                own_top = own_stats[group, pl.ds(local, 1)]
                top = jnp.maximum(part_top, own_top)
                part_share = jnp.exp(part_top - top) * stats[group, pl.ds(PAIR + local, 1)]
                own_share = jnp.exp(own_top - top)
                total = part_share + own_share * own_stats[group, pl.ds(PAIR + local, 1)]
                weighted = part[cols].astype(jnp.float32) * part_share + own[cols] * own_share
                high[cols] = (weighted / total).astype(jnp.bfloat16)

        def step(group):
            make_high(group)
            move_high(group - 1).start()

        each(0, groups, make_own)
        make_high(0)
        each(1, groups, step)
        mask_grad()
        move_high(groups - 1).start()
        wait_rest()

        def finish(group):
            move_low(group).wait_recv()
            update(group)

        each(0, groups, finish)

        def drain(group):
            move_queries(group).wait_send()
            move_high(group).wait_send()

        each(0, groups, drain)

    def drain_trades(group):
        trade_tracker(group).wait_send()
        trade_params(group).wait_send()

    each(0, groups, drain_trades)


def flush_kernel(tracker_ref, params_ref, tracker_out, params_out, sems):
    copies = [
        pltpu.make_async_copy(tracker_ref, tracker_out, sems.at[0]),
        pltpu.make_async_copy(params_ref, params_out, sems.at[1]),
    ]
    for copy in copies:
        copy.start()
    for copy in copies:
        copy.wait()


def flush(tracker, params):
    shape = jax.ShapeDtypeStruct(tracker.shape, tracker.dtype)
    return pl.pallas_call(
        flush_kernel,
        in_specs=[pl.BlockSpec(memory_space=pltpu.VMEM)] * 2,
        out_specs=[pl.BlockSpec(memory_space=pl.ANY)] * 2,
        out_shape=[shape, shape],
        scratch_shapes=[pltpu.SemaphoreType.DMA((2,))],
        compiler_params=pltpu.CompilerParams(vmem_limit_bytes=FLUSH_LIMIT),
        cost_estimate=pl.CostEstimate(
            flops=0, bytes_accessed=2 * tracker.nbytes, transcendentals=0
        ),
    )(tracker, params)


def core_pair_step(queries, keys, values, scales, length, out_grad, params, tracker, old_grad):
    rows, width = queries.shape
    cols = params.shape[1]
    groups = width // GROUP
    smem = pl.BlockSpec(memory_space=pltpu.SMEM)
    anywhere = pl.BlockSpec(memory_space=pl.ANY)
    whole = pl.BlockSpec(memory_space=pltpu.VMEM)
    square = pltpu.VMEM((width, cols), jnp.bfloat16)
    block = pltpu.VMEM((rows, width), jnp.bfloat16)
    turned = pltpu.VMEM((width, rows), jnp.bfloat16)
    stats = pltpu.VMEM((groups, 8, rows), jnp.float32)
    sems = pltpu.SemaphoreType.DMA
    shape = jax.ShapeDtypeStruct((width, cols), jnp.bfloat16)
    done = pl.pallas_call(
        core_pair_kernel,
        in_specs=[smem, smem] + [anywhere] * 7,
        out_specs=[whole, whole],
        out_shape=[shape, shape],
        scratch_shapes=[
            block, block, block, pltpu.VMEM(out_grad.shape, jnp.bfloat16),
            square, square, square, square, square,
            block, turned, turned, turned, stats,
            pltpu.VMEM((width, rows), jnp.float32), stats,
            sems((7,)), sems((2, groups)), sems((2, groups)),
        ] + [sems((groups,))] * 10,
        compiler_params=pltpu.CompilerParams(
            collective_id=0, has_side_effects=True, vmem_limit_bytes=VMEM_LIMIT
        ),
        cost_estimate=pl.CostEstimate(
            flops=4 * width * rows * cols + 12 * rows * rows * width,
            bytes_accessed=14 * width * cols,
            transcendentals=2 * rows * rows * width // HD,
        ),
    )(length.astype(jnp.int32)[None], scales, queries, keys, values, out_grad, tracker, params,
      old_grad)
    return flush(*done)


def step_with(bit_number):
    def step(
        queries, key_store, value_store, kv_exponents, valid_length,
        out_grad, params, tracker, old_grad,
    ):
        if bit_number == 0 and lax.axis_size("ctx") == 2:
            new_tracker, new_params = core_pair_step(
                queries[0], key_store[0], value_store[0],
                jnp.exp2(kv_exponents[0].astype(jnp.float32)), valid_length[0],
                out_grad[0], params[0], tracker[0], old_grad[0],
            )
            return (new_params[None], new_tracker[None])
        split = params.shape[1] - LAST_ROWS
        peer_tracker = from_partner(tracker[0], "dp", bit_number)
        peer_most = from_partner(params[0, :split], "dp", bit_number)
        peer_last = from_partner(params[0, split:], "dp", bit_number)
        length = valid_length[0]
        seq_rows = out_grad.shape[1]
        live_rows = jnp.arange(seq_rows)[:, None] < length
        masked = jnp.where(live_rows, out_grad[0], jnp.zeros((), jnp.bfloat16))
        groups = 2 if lax.axis_size("ctx") == 2 else 1
        exponents = gather_ctx(kv_exponents[0], 0)
        scales = jnp.exp2(exponents.astype(jnp.float32))
        pieces = []
        for group in range(groups):
            pieces.append(
                [
                    rows_to_heads(block[0], group, groups)
                    for block in (key_store, value_store, queries)
                ]
            )
        mine = lax.axis_index("ctx")
        group_heads = HEADS // (lax.axis_size("ctx") * groups)
        width = group_heads * HD
        own_parts = [
            attend(rows, keys, values, scales, length, (mine * groups + group) * group_heads)
            for group, (keys, values, rows) in enumerate(pieces)
        ]
        parts = [gather_ctx(own, 1) for own in own_parts]
        if groups == 1:
            attended = parts[0]
        else:
            attended = jnp.concatenate(
                [
                    part[:, side * width : (side + 1) * width]
                    for side in range(2)
                    for part in parts
                ],
                axis=1,
            )
        grad_new = contract_rows(attended, masked)
        tracker_sum = (
            0.5 * (tracker[0].astype(jnp.float32) + peer_tracker.astype(jnp.float32))
            + grad_new
            - old_grad[0].astype(jnp.float32)
        )
        new_tracker = tracker_sum.astype(jnp.bfloat16)
        new_params = average_rows(params[0], peer_most, new_tracker, 0)
        new_params = average_rows(params[0], peer_last, new_tracker, split, new_params)
        return (new_params[None], new_tracker[None])

    return step


def shards(
    queries,
    key_store,
    value_store,
    kv_exponents,
    valid_length,
    round_index,
    out_grad,
    params,
    tracker,
    old_grad,
):
    levels = lax.axis_size("dp").bit_length() - 1
    bit_now = round_index[0] % levels
    return lax.switch(
        bit_now,
        [step_with(bit_number) for bit_number in range(levels)],
        queries, key_store, value_store, kv_exponents, valid_length,
        out_grad, params, tracker, old_grad,
    )


def solution(mesh):
    placed = (
        P("dp", "ctx", None),
        P("dp", "ctx", None),
        P("dp", "ctx", None),
        P("dp", "ctx", None),
        P("dp"),
        P(),
        P("dp", None, "ctx"),
        P("dp", None, "ctx"),
        P("dp", None, "ctx"),
        P("dp", None, "ctx"),
    )
    return jax.shard_map(
        shards,
        mesh=mesh,
        in_specs=placed,
        out_specs=(P("dp", None, "ctx"), P("dp", None, "ctx")),
        check_vma=False,
    )
```

```python
import functools

import jax
import jax.numpy as jnp
from jax import lax
from jax.experimental import pallas as pl
from jax.experimental.pallas import tpu as pltpu
from jax.sharding import PartitionSpec as P


HEADS = 16
HD = 128
KBLK = 128
QROWS = 256
PIECES = ((384, 384), (64, 64), (64, 64))
MOST_TILE = 256
VMEM_LIMIT = 40 * 2**20
FLUSH_LIMIT = 16 * 2**20
AVERAGE_LIMIT = 16 * 2**20


step_size = 0.1
masked_score = -1e30


def from_partner(value, axis, bit):
    mask = 2**bit
    pairs = [(source, source ^ mask) for source in range(lax.axis_size(axis))]
    return lax.ppermute(value, axis, pairs)


def contract_rows(left_rows, right_rows):
    return lax.dot_general(
        left_rows, right_rows, (((0,), (0,)), ((), ())), preferred_element_type=jnp.float32
    )


def from_other(block):
    return lax.ppermute(block, "ctx", [(0, 1), (1, 0)])


def in_order(own, other, axis):
    first = lax.axis_index("ctx") == 0
    return jnp.concatenate(
        (jnp.where(first, own, other), jnp.where(first, other, own)), axis=axis
    )


def gather_ctx(block, axis):
    if lax.axis_size("ctx") != 2:
        return lax.all_gather(block, "ctx", axis=axis, tiled=True)
    return in_order(block, from_other(block), axis)


def rows_to_heads(block, group, groups):
    if lax.axis_size("ctx") != 2:
        return lax.all_to_all(block, "ctx", split_axis=1, concat_axis=0, tiled=True)
    width = block.shape[1] // (2 * groups)
    mine = lax.axis_index("ctx")
    kept = lax.dynamic_slice_in_dim(block, (mine * groups + group) * width, width, 1)
    sent = lax.dynamic_slice_in_dim(block, ((1 - mine) * groups + group) * width, width, 1)
    return in_order(kept, from_other(sent), 0)


def attend_kernel(step_heads, meta, scales, q_ref, k_ref, v_ref, out_ref):
    length = meta[0]
    seq = k_ref.shape[0]
    for local in range(step_heads):
        head = meta[1] + pl.program_id(0) * step_heads + local
        cols = pl.ds(local * HD, HD)

        def scaled(ref):
            return jnp.concatenate(
                [
                    (
                        ref[pl.ds(block * KBLK, KBLK), cols].astype(jnp.float32)
                        * scales[block, head]
                    ).astype(jnp.bfloat16)
                    for block in range(seq // KBLK)
                ],
                axis=0,
            )

        keys, values = scaled(k_ref), scaled(v_ref)
        for row0 in range(0, seq, QROWS):
            reach = row0 + QROWS
            scores = lax.dot_general(
                q_ref[pl.ds(row0, QROWS), cols],
                keys[:reach],
                (((1,), (1,)), ((), ())),
                preferred_element_type=jnp.float32,
            ) * (HD ** (-0.5))
            query_pos = row0 + lax.broadcasted_iota(jnp.int32, scores.shape, 0)
            key_pos = lax.broadcasted_iota(jnp.int32, scores.shape, 1)
            allowed = (key_pos <= query_pos) & (key_pos < length)
            scores = jnp.where(allowed, scores, masked_score)
            top = jnp.max(scores, axis=-1, keepdims=True)
            weights = jnp.exp(scores - top)
            total = jnp.sum(weights, axis=-1, keepdims=True)
            weighted = jnp.dot(
                weights.astype(jnp.bfloat16), values[:reach], preferred_element_type=jnp.float32
            )
            out_ref[pl.ds(row0, QROWS), cols] = (weighted / total).astype(jnp.bfloat16)


def attend(queries, keys, values, scales, length, first_head):
    seq, width = queries.shape
    heads = width // HD
    step_heads = 2 if heads % 2 == 0 and seq <= 512 else 1
    meta = jnp.stack((length, first_head)).astype(jnp.int32)
    spec = pl.BlockSpec((seq, step_heads * HD), lambda h: (0, h))
    smem = pl.BlockSpec(memory_space=pltpu.SMEM)
    return pl.pallas_call(
        functools.partial(attend_kernel, step_heads),
        grid=(heads // step_heads,),
        in_specs=[smem, smem, spec, spec, spec],
        out_specs=spec,
        out_shape=jax.ShapeDtypeStruct((seq, width), jnp.bfloat16),
        cost_estimate=pl.CostEstimate(
            flops=4 * seq * seq * width,
            bytes_accessed=8 * seq * width,
            transcendentals=seq * seq * heads,
        ),
    )(meta, scales, queries, keys, values)


def average_kernel(own_ref, peer_ref, tracker_ref, *rest):
    out_ref = rest[-1]
    out_ref[...] = (
        0.5 * (own_ref[...].astype(jnp.float32) + peer_ref[...].astype(jnp.float32))
        - step_size * tracker_ref[...].astype(jnp.float32)
    ).astype(jnp.bfloat16)


def average_rows(own, peer_rows, new_tracker, start, tile, filled=None):
    rows, cols = peer_rows.shape
    here = pl.BlockSpec((tile, cols), lambda i: (i + start // tile, 0))
    operands = [own, peer_rows, new_tracker]
    peer_spec = pl.BlockSpec((tile, cols), lambda i: (i, 0))
    specs = [here, peer_spec, here]
    aliases = {}
    if filled is not None:
        operands.append(filled)
        specs.append(pl.BlockSpec(memory_space=pl.ANY))
        aliases = {3: 0}
    return pl.pallas_call(
        average_kernel,
        grid=(rows // tile,),
        in_specs=specs,
        out_specs=here,
        out_shape=jax.ShapeDtypeStruct(own.shape, jnp.bfloat16),
        input_output_aliases=aliases,
        compiler_params=pltpu.CompilerParams(vmem_limit_bytes=AVERAGE_LIMIT),
        cost_estimate=pl.CostEstimate(
            flops=4 * rows * cols, bytes_accessed=8 * rows * cols, transcendentals=0
        ),
    )(*operands)


PAIR = 2
GROUP = PAIR * HD
MESH = pl.DeviceIdType.MESH


def power_of_two(exponent):
    return jnp.where(exponent > 0, 2.0, jnp.where(exponent < 0, 0.5, 1.0)).astype(jnp.float32)


def scaled_rows(ref, scales, head, cols):
    return jnp.concatenate(
        [
            (
                ref[pl.ds(block * KBLK, KBLK), cols].astype(jnp.float32)
                * power_of_two(scales[block, head])
            ).astype(jnp.bfloat16)
            for block in range(ref.shape[0] // KBLK)
        ],
        axis=0,
    )


def attend_columns(queries, keys, values, allowed):
    scores = lax.dot_general(
        keys, queries, (((1,), (1,)), ((), ())), preferred_element_type=jnp.float32
    ) * (HD ** (-0.5))
    scores = jnp.where(allowed, scores, masked_score)
    top = jnp.max(scores, axis=0, keepdims=True)
    weights = jnp.exp(scores - top)
    total = jnp.sum(weights, axis=0, keepdims=True)
    return contract_rows(values, weights.astype(jnp.bfloat16)), top, total


def core_pair_kernel(
    length_ref, scales, query_hbm, key_hbm, value_hbm, grad_hbm, tracker_hbm, params_hbm, old_hbm,
    new_tracker_ref, new_params_ref,
    queries, keys, values, masked, tracker, params, old, peer_tracker, peer_params,
    peer_queries, low, high, part, stats, own, own_stats, base, average,
    load_sem, trade_send, trade_recv, query_send, query_recv, low_send, low_recv,
    high_send, high_recv, part_send, part_recv, stats_send, stats_recv,
):
    rows = queries.shape[0]
    groups = queries.shape[1] // GROUP
    side = lax.axis_index("ctx")
    place = lax.axis_index("dp")
    across = {"ctx": 1 - side}
    partner = {"dp": place + 1 - 2 * (place % 2)}
    length = length_ref[0]

    def span(group):
        return pl.ds(pl.multiple_of(group * GROUP, GROUP), GROUP)

    def remote(source, target, send, recv, device):
        return pltpu.make_async_remote_copy(
            src_ref=source, dst_ref=target, send_sem=send, recv_sem=recv,
            device_id=device, device_id_type=MESH,
        )

    def trade_tracker(group):
        here = span(group)
        return remote(tracker_hbm.at[here], peer_tracker.at[here],
                      trade_send.at[0, group], trade_recv.at[0, group], partner)

    def trade_params(group):
        here = span(group)
        return remote(params_hbm.at[here], peer_params.at[here],
                      trade_send.at[1, group], trade_recv.at[1, group], partner)

    def move_queries(group):
        here = span(group)
        return remote(query_hbm.at[:, here], peer_queries.at[:, here],
                      query_send.at[group], query_recv.at[group], across)

    def move_low(group):
        here = span(group)
        return remote(low.at[here], low.at[here], low_send.at[group], low_recv.at[group], across)

    def move_high(group):
        here = span(group)
        return remote(high.at[here], high.at[here], high_send.at[group], high_recv.at[group],
                      across)

    def move_part(group):
        here = span(group)
        return remote(part.at[here], part.at[here], part_send.at[group], part_recv.at[group],
                      across)

    def move_stats(group):
        return remote(stats.at[group], stats.at[group], stats_send.at[group],
                      stats_recv.at[group], across)

    loads = [
        pltpu.make_async_copy(source, target, load_sem.at[index])
        for index, (source, target) in enumerate((
            (query_hbm, queries), (key_hbm, keys), (value_hbm, values), (grad_hbm, masked),
            (tracker_hbm, tracker), (params_hbm, params), (old_hbm, old),
        ))
    ]
    for load in loads[:3]:
        load.start()
    barrier = pltpu.get_barrier_semaphore()
    for device in (across, partner):
        pl.semaphore_signal(barrier, inc=1, device_id=device, device_id_type=MESH)

    def each(first, last, body):
        def step(group, carry):
            body(group)
            return carry

        lax.fori_loop(first, last, step, 0)

    key_pos = lax.broadcasted_iota(jnp.int32, (rows, rows), 0)
    query_pos = lax.broadcasted_iota(jnp.int32, (rows, rows), 1)

    def heads_of(group):
        for local in range(PAIR):
            head = group * PAIR + local
            yield local, head, pl.ds(pl.multiple_of(head * HD, HD), HD)

    def own_keys(head, cols):
        return scaled_rows(keys, scales, head, cols), scaled_rows(values, scales, head, cols)

    def lanes(index):
        return pl.ds(index * rows, rows)

    def mask_grad():
        loads[3].wait()
        for block in range(masked.shape[0] // KBLK):
            here = pl.ds(block * KBLK, KBLK)
            position = block * KBLK + lax.broadcasted_iota(jnp.int32, (KBLK, masked.shape[1]), 0)
            masked[here] = jnp.where(
                position < length, masked[here].astype(jnp.float32), 0.0
            ).astype(jnp.bfloat16)

    def grad_part(block, group, first_row):
        return jnp.dot(
            block[span(group)], masked[pl.ds(first_row, rows)], preferred_element_type=jnp.float32
        )

    def update(group, known, known_row, arriving, arriving_row, arrival):
        here = span(group)
        trade_tracker(group).wait_recv()
        trade_params(group).wait_recv()
        base[...] = (
            0.5 * (tracker[here].astype(jnp.float32) + peer_tracker[here].astype(jnp.float32))
            + grad_part(known, group, known_row)
            - old[here].astype(jnp.float32)
        )
        average[...] = 0.5 * (
            params[here].astype(jnp.float32) + peer_params[here].astype(jnp.float32)
        )
        arrival.wait_recv()
        new_tracker = (base[...] + grad_part(arriving, group, arriving_row)).astype(jnp.bfloat16)
        new_tracker_ref[here] = new_tracker
        new_params_ref[here] = (
            average[...] - step_size * new_tracker.astype(jnp.float32)
        ).astype(jnp.bfloat16)

    def wait_rest():
        for load in loads[4:]:
            load.wait()

    def make_low(group):
        for _, head, cols in heads_of(group):
            head_keys, head_values = own_keys(head, cols)
            weighted, _, total = attend_columns(
                queries[:, cols], head_keys, head_values, (key_pos <= query_pos) & (key_pos < length)
            )
            low[cols] = (weighted / total).astype(jnp.bfloat16)

    @pl.when(side == 0)
    def _():
        for load in loads[:3]:
            load.wait()
        make_low(0)

    pl.semaphore_wait(barrier, 2)

    @pl.when(side == 0)
    def _():
        move_low(0).start()

    @pl.when(side == 1)
    def _():
        each(0, groups, lambda group: move_queries(group).start())

    def start_trades(group):
        trade_tracker(group).start()
        trade_params(group).start()

    each(0, groups, start_trades)
    for load in loads[3:]:
        load.start()

    @pl.when(side == 1)
    def _():
        for load in loads[:3]:
            load.wait()

    @pl.when(side == 0)
    def _():
        live = key_pos < length

        def make_part(group):
            move_queries(group).wait_recv()
            for local, head, cols in heads_of(group):
                head_keys, head_values = own_keys(head, cols)
                weighted, top, total = attend_columns(
                    peer_queries[:, cols], head_keys, head_values, live
                )
                part[cols] = (weighted / total).astype(jnp.bfloat16)
                stats[group, :, lanes(local)] = top
                stats[group, :, lanes(PAIR + local)] = total

        def send_part(group):
            move_part(group).start()
            move_stats(group).start()

        def step(group):
            make_part(group)
            make_low(group + 2)
            send_part(group)

        make_low(1)
        move_low(1).start()
        each(0, groups - 2, step)
        make_part(groups - 2)
        send_part(groups - 2)
        make_part(groups - 1)
        mask_grad()
        send_part(groups - 1)
        each(2, groups, lambda group: move_low(group).start())
        wait_rest()

        def finish(group):
            update(group, low, 0, high, rows, move_high(group))

        each(0, groups, finish)

        def drain(group):
            move_low(group).wait_send()
            move_part(group).wait_send()
            move_stats(group).wait_send()

        each(0, groups, drain)

    @pl.when(side == 1)
    def _():
        causal = (key_pos <= query_pos) & (key_pos + rows < length)

        def make_own(group):
            for local, head, cols in heads_of(group):
                head_keys, head_values = own_keys(head, cols)
                weighted, top, total = attend_columns(
                    queries[:, cols], head_keys, head_values, causal
                )
                own[cols] = weighted
                own_stats[group, :, lanes(local)] = top
                own_stats[group, :, lanes(PAIR + local)] = total

        def make_high(group):
            move_part(group).wait_recv()
            move_stats(group).wait_recv()
            for local, _, cols in heads_of(group):
                part_top = stats[group, :, lanes(local)]
                own_top = own_stats[group, :, lanes(local)]
                top = jnp.maximum(part_top, own_top)
                part_share = jnp.exp(part_top - top) * stats[group, :, lanes(PAIR + local)]
                own_share = jnp.exp(own_top - top)
                total = part_share + own_share * own_stats[group, :, lanes(PAIR + local)]
                weighted = part[cols].astype(jnp.float32) * part_share + own[cols] * own_share
                high[cols] = (weighted / total).astype(jnp.bfloat16)

        def step(group):
            make_high(group)
            move_high(group - 1).start()

        each(0, groups, make_own)
        make_high(0)
        each(1, groups, step)
        mask_grad()
        move_high(groups - 1).start()
        wait_rest()

        def finish(group):
            update(group, high, rows, low, 0, move_low(group))

        each(0, groups, finish)

        def drain(group):
            move_queries(group).wait_send()
            move_high(group).wait_send()

        each(0, groups, drain)

    def drain_trades(group):
        trade_tracker(group).wait_send()
        trade_params(group).wait_send()

    each(0, groups, drain_trades)


def flush_kernel(tracker_ref, params_ref, tracker_out, params_out, sems):
    copies = [
        pltpu.make_async_copy(tracker_ref, tracker_out, sems.at[0]),
        pltpu.make_async_copy(params_ref, params_out, sems.at[1]),
    ]
    for copy in copies:
        copy.start()
    for copy in copies:
        copy.wait()


def flush(tracker, params):
    shape = jax.ShapeDtypeStruct(tracker.shape, tracker.dtype)
    return pl.pallas_call(
        flush_kernel,
        in_specs=[pl.BlockSpec(memory_space=pltpu.VMEM)] * 2,
        out_specs=[pl.BlockSpec(memory_space=pl.ANY)] * 2,
        out_shape=[shape, shape],
        scratch_shapes=[pltpu.SemaphoreType.DMA((2,))],
        compiler_params=pltpu.CompilerParams(vmem_limit_bytes=FLUSH_LIMIT),
        cost_estimate=pl.CostEstimate(
            flops=0, bytes_accessed=2 * tracker.nbytes, transcendentals=0
        ),
    )(tracker, params)


def core_pair_step(queries, keys, values, scales, length, out_grad, params, tracker, old_grad):
    rows, width = queries.shape
    cols = params.shape[1]
    groups = width // GROUP
    smem = pl.BlockSpec(memory_space=pltpu.SMEM)
    anywhere = pl.BlockSpec(memory_space=pl.ANY)
    whole = pl.BlockSpec(memory_space=pltpu.VMEM)
    square = pltpu.VMEM((width, cols), jnp.bfloat16)
    block = pltpu.VMEM((rows, width), jnp.bfloat16)
    turned = pltpu.VMEM((width, rows), jnp.bfloat16)
    stats = pltpu.VMEM((groups, 1, 2 * PAIR * rows), jnp.float32)
    sems = pltpu.SemaphoreType.DMA
    shape = jax.ShapeDtypeStruct((width, cols), jnp.bfloat16)
    done = pl.pallas_call(
        core_pair_kernel,
        in_specs=[smem, smem] + [anywhere] * 7,
        out_specs=[whole, whole],
        out_shape=[shape, shape],
        scratch_shapes=[
            block, block, block, pltpu.VMEM(out_grad.shape, jnp.bfloat16),
            square, square, square, square, square,
            block, turned, turned, turned, stats,
            pltpu.VMEM((width, rows), jnp.float32), stats,
            pltpu.VMEM((GROUP, cols), jnp.float32), pltpu.VMEM((GROUP, cols), jnp.float32),
            sems((7,)), sems((2, groups)), sems((2, groups)),
        ] + [sems((groups,))] * 10,
        compiler_params=pltpu.CompilerParams(
            collective_id=0, has_side_effects=True, vmem_limit_bytes=VMEM_LIMIT
        ),
        cost_estimate=pl.CostEstimate(
            flops=4 * width * rows * cols + 12 * rows * rows * width,
            bytes_accessed=14 * width * cols,
            transcendentals=2 * rows * rows * width // HD,
        ),
    )(length.astype(jnp.int32)[None], scales, queries, keys, values, out_grad, tracker, params,
      old_grad)
    return flush(*done)


def step_with(bit_number):
    def step(
        queries, key_store, value_store, kv_exponents, valid_length,
        out_grad, params, tracker, old_grad,
    ):
        if bit_number == 0 and lax.axis_size("ctx") == 2:
            new_tracker, new_params = core_pair_step(
                queries[0], key_store[0], value_store[0],
                kv_exponents[0], valid_length[0],
                out_grad[0], params[0], tracker[0], old_grad[0],
            )
            return (new_params[None], new_tracker[None])
        pieces_at = []
        start = params.shape[1] - sum(rows for rows, _ in PIECES)
        pieces_at.append((0, start, MOST_TILE))
        for rows, tile in PIECES:
            pieces_at.append((start, rows, tile))
            start += rows
        peer_tracker = from_partner(tracker[0], "dp", bit_number)
        peer_pieces = []
        for start, rows, _ in pieces_at:
            peer_pieces.append(
                from_partner(params[0, start : start + rows], "dp", bit_number)
            )
        length = valid_length[0]
        seq_rows = out_grad.shape[1]
        live_rows = jnp.arange(seq_rows)[:, None] < length
        masked = jnp.where(live_rows, out_grad[0], jnp.zeros((), jnp.bfloat16))
        groups = 2 if lax.axis_size("ctx") == 2 else 1
        exponents = gather_ctx(kv_exponents[0], 0)
        scales = jnp.exp2(exponents.astype(jnp.float32))
        pieces = []
        for group in range(groups):
            pieces.append(
                [
                    rows_to_heads(block[0], group, groups)
                    for block in (key_store, value_store, queries)
                ]
            )
        mine = lax.axis_index("ctx")
        group_heads = HEADS // (lax.axis_size("ctx") * groups)
        width = group_heads * HD
        own_parts = [
            attend(rows, keys, values, scales, length, (mine * groups + group) * group_heads)
            for group, (keys, values, rows) in enumerate(pieces)
        ]
        parts = [gather_ctx(own, 1) for own in own_parts]
        if groups == 1:
            attended = parts[0]
        else:
            attended = jnp.concatenate(
                [
                    part[:, side * width : (side + 1) * width]
                    for side in range(2)
                    for part in parts
                ],
                axis=1,
            )
        grad_new = contract_rows(attended, masked)
        tracker_sum = (
            0.5 * (tracker[0].astype(jnp.float32) + peer_tracker.astype(jnp.float32))
            + grad_new
            - old_grad[0].astype(jnp.float32)
        )
        new_tracker = tracker_sum.astype(jnp.bfloat16)
        new_params = None
        for (start, _, tile), peer_rows in zip(pieces_at, peer_pieces):
            new_params = average_rows(params[0], peer_rows, new_tracker, start, tile, new_params)
        return (new_params[None], new_tracker[None])

    return step


def shards(
    queries,
    key_store,
    value_store,
    kv_exponents,
    valid_length,
    round_index,
    out_grad,
    params,
    tracker,
    old_grad,
):
    levels = lax.axis_size("dp").bit_length() - 1
    bit_now = round_index[0] % levels
    return lax.switch(
        bit_now,
        [step_with(bit_number) for bit_number in range(levels)],
        queries, key_store, value_store, kv_exponents, valid_length,
        out_grad, params, tracker, old_grad,
    )


def solution(mesh):
    placed = (
        P("dp", "ctx", None),
        P("dp", "ctx", None),
        P("dp", "ctx", None),
        P("dp", "ctx", None),
        P("dp"),
        P(),
        P("dp", None, "ctx"),
        P("dp", None, "ctx"),
        P("dp", None, "ctx"),
        P("dp", None, "ctx"),
    )
    return jax.shard_map(
        shards,
        mesh=mesh,
        in_specs=placed,
        out_specs=(P("dp", None, "ctx"), P("dp", None, "ctx")),
        check_vma=False,
    )
```
